32 devices in a mesh: fsdp: 4 (over y, x), grp: 8 (over z, core).
Axes of the slice: x: 2, y: 2, z: 4, core: 2. Of those that a mesh axis runs over, the one named last changes fastest.
Arguments:
- grad_out: bfloat16 [32, 512, 512], P(('fsdp', 'grp')), may hold values from -6 to 6
- pre_first: bfloat16 [32, 512, 512], P(('fsdp', 'grp')), may hold values from -8 to 8
- pre_second: bfloat16 [32, 512, 512], P(('fsdp', 'grp')), may hold values from -8 to 8
- conv_first: bfloat16 [3, 512, 512], P(None, 'fsdp'), may hold values from -0.15625 to 0.15625
- conv_second: bfloat16 [3, 512, 512], P(None, 'fsdp'), may hold values from -0.15625 to 0.15625
- lengths: int32 [32], P(('fsdp', 'grp')), may hold values from 64 to 512
- item_ids: int32 [16384], P('grp'), may hold values from 0 to 8191
- owners: int32 [512, 1], P('grp'), may hold values from 0 to 7; in each aligned block of 64 rows (0 to 63, 64 to 127, ...) at most 16 rows name the same one
Outputs:
- table_grad: float32 [512, 65536], P('fsdp', 'grp')
The draws below stay inside these ranges and needn't reach their ends.
Inputs may be any that keep to these rules, and one draw needn't show every extreme that they name: `owners`: among the blocks of one group, no owner is named by more than 16 blocks, a bound that some block reaches.
All inputs are finite; a program needn't handle non-finite values.
Results may differ from the reference program's by a relative error of at most 0.0037.
Values may be sent and summed in bfloat16 or wider, within the bound.
A program may use at most 64 MiB of HBM per device.

```python
import math
import jax
import jax.numpy as jnp
import numpy as np
from jax import lax

D = 512
L = 512
BLK = 32
ROWS_OWN = 8192
USERS = 32
GROUP_ROWS = 2048
BLOCKS_GRP = 64
CAP = 16
TABLE_ROWS = 65536
N_FSDP = 4
N_GRP = 8


def touch_ends(result, stream_key, low, top_value):
    extent = result.shape
    spot = [jax.random.randint(jax.random.fold_in(stream_key, axis), (), 0, extent[axis]) for axis in range(len(extent))]
    result = result.at[tuple(spot)].set(low)
    longest = extent.index(max(extent))
    spot[longest] = (spot[longest] + 1) % extent[longest]
    return result.at[tuple(spot)].set(top_value)


def block_scale(stream_key, shape, split, least, high):
    factor_of, own = 1.0, jax.random.fold_in(stream_key, 6)
    for axis_at, blocks in split:
        heights = jnp.exp(jax.random.uniform(jax.random.fold_in(own, axis_at), (blocks,), jnp.float32, least / len(split), high / len(split)))
        factor_of = factor_of * jnp.repeat(heights, shape[axis_at] // blocks).reshape([-1 if axis == axis_at else 1 for axis in range(len(shape))])
    return factor_of


def rank_bounds(number_of, slope):
    weights = [(1 << 20) // math.isqrt(rank ** slope) + 1 for rank in range(1, number_of + 1)]
    spread = 1 + sum(weights) // (1 << 30)
    return np.cumsum(np.array([max(1, weight // spread) for weight in weights]))


def ranked(own_key, extent, number_of, skew):
    grid = rank_bounds(number_of, skew)
    ticket = jax.random.randint(jax.random.fold_in(own_key, 1), extent, 0, int(grid[number_of - 1]))
    standing = jnp.searchsorted(jnp.asarray(grid, jnp.int32), ticket, side="right")
    return jax.random.permutation(jax.random.fold_in(own_key, 2), number_of)[standing].astype(jnp.int32)


def deal_out(own_key, own, number, rows, count, top, most, slope):
    order = jax.random.permutation(own_key, count)
    crowded, ordinary = shares(count, rows * top, most, slope, True), shares(count, rows * top, most, slope, False)
    places = jnp.arange(count)

    def named(sizes, turn):
        used = int((sizes > 0).sum())
        fixed = max(1, used // 4)
        shifted = fixed + (places - fixed + turn * (used - fixed)) % max(1, count - fixed)
        return jnp.zeros((count,), jnp.int32).at[order[jnp.where(places < fixed, places, shifted)]].set(jnp.asarray(sizes, jnp.int32))

    sizes = jnp.where(number % 4 == 0, named(crowded, number // 4), named(ordinary, number - number // 4 - 1))
    mixed = jax.random.permutation(jax.random.fold_in(own, 3), count)
    giver, sink = mixed[0:count // 2 * 2:2], mixed[1:count // 2 * 2:2]
    room = jnp.minimum(sizes[giver] - 1, most - sizes[sink]) // 2
    room = jnp.where((giver == order[0]) | (sink == order[0]) | (sizes[sink] == 0), 0, jnp.maximum(room, 0))
    shifted = jax.random.randint(jax.random.fold_in(own, 4), (count // 2,), 0, 1 << 20) % (room + 1)
    sizes = sizes.at[giver].add(-shifted).at[sink].add(shifted)
    members = jnp.searchsorted(jnp.cumsum(sizes), jnp.arange(rows * top), side="right").astype(jnp.int32)
    listing = members.reshape(top, rows).T
    listing = listing[jax.random.permutation(jax.random.fold_in(own, 1), rows)]
    turn = jax.random.randint(jax.random.fold_in(own, 2), (rows, 1), 0, top)
    return jnp.take_along_axis(listing, (jnp.arange(top)[None, :] + turn) % top, axis=1)


def shares(count, total, reach, lean, full):
    loads = [(1 << 20) // math.isqrt(rank ** lean) + 1 for rank in range(1, count + 1)]
    largest = reach if full else min(reach, max(-(-total // count), total * loads[0] // sum(loads)))
    least = 1 if total - largest >= count - 1 else 0
    given, spare = [largest] + [least] * (count - 1), total - largest - least * (count - 1)
    while spare > 0:
        movable = [i for i in range(1, count) if given[i] < largest] or [i for i in range(1, count) if given[i] < reach]
        whole, left = sum([loads[i] for i in movable]), spare
        for i in movable:
            more = min(reach - given[i], max(1, left * loads[i] // whole), spare)
            given[i] = given[i] + more
            spare = spare - more
    return np.array(given)


def bell_draw(key, shape, scale, most, cuts=(), kind=jnp.bfloat16):
    entries = jax.random.normal(key, shape, jnp.float32) * scale
    if len(cuts) > 0:
        entries = block_scale(key, shape, cuts, -0.22, 0.18) * entries
    return jnp.clip(entries, min=-most, max=most).astype(kind)


def setup_inputs(seed: int = 0) -> dict:
    seeds = jax.random.split(jax.random.key(seed), 9)
    grad_out = bell_draw(seeds[0], (USERS, L, D), 1.0, 6.0, ((0, 32),))
    pre_first = bell_draw(seeds[1], (USERS, L, D), 1.5, 8.0, ((0, 32),))
    pre_second = bell_draw(seeds[2], (USERS, L, D), 1.5, 8.0, ((0, 32),))
    conv_first = bell_draw(seeds[3], (3, D, D), (3 * D) ** -0.5, 0.15625, ((1, 4),))
    conv_second = bell_draw(seeds[4], (3, D, D), (3 * D) ** -0.5, 0.15625, ((1, 4),))
    lengths = touch_ends(jax.random.randint(seeds[5], (USERS,), L // 8, L + 1), jax.random.fold_in(seeds[5], 1), L // 8, L).astype(jnp.int32)
    item_ids = touch_ends(ranked(seeds[6], (N_GRP * GROUP_ROWS,), ROWS_OWN, 2), jax.random.fold_in(seeds[6], 3), 0, ROWS_OWN - 1).astype(jnp.int32)
    owners_keys = jax.random.split(jax.random.fold_in(seeds[7], 1), (N_GRP * BLOCKS_GRP) // BLOCKS_GRP)
    owners_turns = jax.random.permutation(jax.random.fold_in(seeds[7], 3), (N_GRP * BLOCKS_GRP) // BLOCKS_GRP)
    owners = jax.vmap(lambda own, number: deal_out(jax.random.fold_in(seeds[7], 2), own, number, BLOCKS_GRP, N_GRP, 1, CAP, 2))(owners_keys, owners_turns).reshape((N_GRP * BLOCKS_GRP, 1))
    return dict(grad_out=grad_out, pre_first=pre_first, pre_second=pre_second, conv_first=conv_first, conv_second=conv_second, lengths=lengths, item_ids=item_ids, owners=owners)


def layer_back(gradient, pre_acts, weights, live_rows, dilation):
    pre_float = pre_acts.astype(jnp.float32)
    sig_val = jax.nn.sigmoid(pre_float)
    deltas = (gradient * sig_val * (1.0 + pre_float * (1.0 - sig_val))).astype(jnp.bfloat16)
    padded = jnp.pad(deltas, ((dilation, dilation), (0, 0)))
    after = padded[2 * dilation:2 * dilation + L]
    middle = padded[dilation:dilation + L]
    before = padded[0:L]
    summed = jnp.dot(after, weights[0].T, preferred_element_type=jnp.float32)
    summed = summed + jnp.dot(middle, weights[1].T, preferred_element_type=jnp.float32)
    summed = summed + jnp.dot(before, weights[2].T, preferred_element_type=jnp.float32)
    return gradient + live_rows * summed


def reference(grad_out, pre_first, pre_second, conv_first, conv_second, lengths, item_ids, owners):
    positions = jnp.arange(L, dtype=jnp.int32)

    def one_user(inputs):
        user_grad, first_acts, second_acts, length = inputs
        live_rows = (positions < length).astype(jnp.float32)[:, None]
        gradient = user_grad.astype(jnp.float32)
        gradient = layer_back(gradient, second_acts, conv_second, live_rows, 2)
        gradient = layer_back(gradient, first_acts, conv_first, live_rows, 1)
        return (live_rows * gradient).astype(jnp.bfloat16)

    row_grad = lax.map(one_user, (grad_out, pre_first, pre_second, lengths))
    row_grad = row_grad.reshape(N_FSDP, N_GRP, L, D).transpose(1, 0, 2, 3).reshape(N_GRP, GROUP_ROWS, D)
    block_owner = jnp.repeat(owners[:, 0].reshape(N_GRP, BLOCKS_GRP), BLK, axis=1)
    table_index = (block_owner * ROWS_OWN + item_ids.reshape(N_GRP, GROUP_ROWS)).astype(jnp.int32)

    def add_group(summed, inputs):
        group_rows, group_index = inputs
        return summed.at[group_index].add(group_rows.astype(jnp.float32)), None

    table = jnp.zeros((TABLE_ROWS, D), jnp.float32)
    table, unused = lax.scan(add_group, table, (row_grad, table_index))
    return table.T
```

```python
import functools

import jax
import jax.numpy as jnp
from jax import lax
from jax.experimental import pallas as pl
from jax.experimental.pallas import tpu as pltpu
from jax.sharding import PartitionSpec as P

MESH = pl.DeviceIdType.MESH
BLK = 32
ROWS_OWN = 8192
PAD = 8
TABLES = 4


def flip(index, mask):
    out = 0
    for bit in range(6):
        have = (index // (1 << bit)) % 2
        out = out + ((1 - have) if (mask >> bit) & 1 else have) * (1 << bit)
    return out


def plan_kernel(slot_cap, own_ref, ids_ref, src_ref, sid_ref, cnt_ref):
    blocks = ids_ref.shape[0]
    slots = sid_ref.shape[0]
    sid_ref[...] = jnp.full(sid_ref.shape, -1, jnp.int32)

    def clear_src(i, c):
        src_ref[i] = 0
        return c

    def clear_cnt(i, c):
        cnt_ref[i] = 0
        return c

    lax.fori_loop(0, slots, clear_src, 0)
    lax.fori_loop(0, slots // slot_cap, clear_cnt, 0)

    def place(b, c):
        owner = own_ref[b]
        rank = cnt_ref[owner]
        cnt_ref[owner] = rank + 1
        slot = owner * slot_cap + rank
        src_ref[slot] = b
        sid_ref[pl.ds(slot, 1), :] = ids_ref[pl.ds(b, 1), :]
        return c

    lax.fori_loop(0, blocks, place, 0)


def exchange_kernel(
    slot_cap,
    owner_count,
    src_ref,
    len_ref,
    ids_ref,
    go_ref,
    p1_ref,
    p2_ref,
    w1_ref,
    w2_ref,
    rows_out,
    ids_out,
    wfull,
    pad,
    dsh,
    grad,
    rg,
    gcols,
    send,
    dir_s,
    dir_r,
    rel_s,
    rel_r,
    fw_s,
    fw_r,
    feat_s,
    feat_r,
    row_s,
    row_r,
    id_s,
    id_r,
):
    f = lax.axis_index("fsdp")
    g = lax.axis_index("grp")
    core = g % 2
    seq = grad.shape[0]
    width = grad.shape[1]
    cols = width // 4
    half = cols // 2
    quarter = cols // 4
    fx, fy, fd = flip(f, 1), flip(f, 2), flip(f, 3)
    mate = flip(g, 1)

    barrier = pltpu.get_barrier_semaphore()
    for peer in (fx, fy, fd):
        pl.semaphore_signal(barrier, inc=1, device_id=(peer, g), device_id_type=MESH)
    for m in range(1, owner_count):
        pl.semaphore_signal(barrier, inc=1, device_id=(f, flip(g, m)), device_id_type=MESH)
    pl.semaphore_wait(barrier, 3 + owner_count - 1)

    w_refs = (w2_ref, w1_ref)

    def part(layer, owner, off, rows):
        return wfull.at[layer, :, pl.ds(pl.multiple_of(owner * cols + off, quarter), rows), :]

    def direct(layer, way, sub):
        peer = (fx, fy)[way]
        off = core * half + sub * quarter
        return pltpu.make_async_remote_copy(
            src_ref=w_refs[layer].at[:, pl.ds(pl.multiple_of(off, quarter), quarter), :],
            dst_ref=part(layer, f, off, quarter),
            send_sem=dir_s.at[layer, way, sub],
            recv_sem=dir_r.at[layer, way, sub],
            device_id=(peer, g),
            device_id_type=MESH,
        )

    def relay(layer, sub):
        holder, peer = ((fx, fy), (fy, fx))[sub]
        place = part(layer, holder, core * half + sub * quarter, quarter)
        return pltpu.make_async_remote_copy(
            src_ref=place,
            dst_ref=place,
            send_sem=rel_s.at[layer, sub],
            recv_sem=rel_r.at[layer, sub],
            device_id=(peer, g),
            device_id_type=MESH,
        )

    def forward(layer, which):
        place = part(layer, (fx, fy, fd)[which], core * half, half)
        return pltpu.make_async_remote_copy(
            src_ref=place,
            dst_ref=place,
            send_sem=fw_s.at[layer, which],
            recv_sem=fw_r.at[layer, which],
            device_id=(f, mate),
            device_id_type=MESH,
        )

    directs = [[[direct(l, w, s) for s in range(2)] for w in range(2)] for l in range(2)]
    relays = [[relay(l, s) for s in range(2)] for l in range(2)]
    forwards = [[forward(l, i) for i in range(3)] for l in range(2)]

    def start_directs(layer):
        directs[layer][0][0].start()
        directs[layer][1][1].start()
        directs[layer][0][1].start()
        directs[layer][1][0].start()

    def start_relays(layer):
        directs[layer][0][0].wait_recv()
        relays[layer][0].start()
        directs[layer][1][1].wait_recv()
        relays[layer][1].start()

    def start_forwards(layer):
        directs[layer][0][1].wait_recv()
        forwards[layer][0].start()
        directs[layer][1][0].wait_recv()
        forwards[layer][1].start()
        relays[layer][0].wait_recv()
        relays[layer][1].wait_recv()
        forwards[layer][2].start()

    def wait_forwards(layer):
        for i in range(3):
            forwards[layer][i].wait_recv()

    start_directs(0)

    id_copies = []
    for m in range(1, owner_count):
        dest = flip(g, m)
        id_copies.append(
            pltpu.make_async_remote_copy(
                src_ref=ids_ref.at[pl.ds(pl.multiple_of(dest * slot_cap, slot_cap), slot_cap), :],
                dst_ref=ids_out.at[pl.ds(pl.multiple_of(g * slot_cap, slot_cap), slot_cap), :],
                send_sem=id_s.at[m - 1],
                recv_sem=id_r.at[m - 1],
                device_id=(f, dest),
                device_id_type=MESH,
            )
        )
        id_copies[-1].start()
    own_ids = pl.ds(pl.multiple_of(g * slot_cap, slot_cap), slot_cap)
    ids_out[own_ids, :] = ids_ref[own_ids, :]

    pad[0:PAD, :] = jnp.zeros((PAD, width), jnp.float32)
    pad[PAD + seq : 2 * PAD + seq, :] = jnp.zeros((PAD, width), jnp.float32)
    own_cols = pl.ds(pl.multiple_of(f * cols, cols), cols)
    wfull[0, :, own_cols, :] = w2_ref[...]
    wfull[1, :, own_cols, :] = w1_ref[...]
    step = 64

    def taps(first, pre_ref, dilation):
        for i in range(seq // step):
            rows = slice(i * step, (i + 1) * step)
            z = pre_ref[rows, :].astype(jnp.float32)
            s = jax.nn.sigmoid(z)
            grad_rows = first[rows, :].astype(jnp.float32)
            d = (grad_rows * s * (1.0 + z * (1.0 - s))).astype(jnp.bfloat16)
            dsh[1, rows, :] = d
            pad[PAD + i * step : PAD + (i + 1) * step, :] = d.astype(jnp.float32)
        for i in range(seq // step):
            rows = slice(i * step, (i + 1) * step)
            low = PAD + i * step
            dsh[0, rows, :] = pad[low + dilation : low + dilation + step, :].astype(jnp.bfloat16)
            dsh[2, rows, :] = pad[low - dilation : low - dilation + step, :].astype(jnp.bfloat16)

    def product(layer, rows, wrows):
        total = None
        for k in range(3):
            one = lax.dot_general(
                dsh[k, rows, :],
                wfull[layer, k, wrows, :],
                (((1,), (1,)), ((), ())),
                preferred_element_type=jnp.float32,
            )
            total = one if total is None else total + one
        return total

    mrows = seq // 2

    def live_of(i):
        spots = lax.broadcasted_iota(jnp.int32, (mrows, 1), 0) + i * mrows
        return (spots < len_ref[0]).astype(jnp.float32)

    taps(go_ref, p2_ref, 2)
    start_relays(0)
    start_directs(1)
    start_forwards(0)
    wait_forwards(0)
    for j in range(2):
        wrows = slice(j * 2 * cols, (j + 1) * 2 * cols)
        for i in range(2):
            rows = slice(i * mrows, (i + 1) * mrows)
            grad[rows, wrows] = go_ref[rows, wrows].astype(jnp.float32) + live_of(i) * product(
                0, rows, wrows
            )
    start_relays(1)
    taps(grad, p1_ref, 1)
    start_forwards(1)
    wait_forwards(1)

    feat_copies = []
    for n, dest in enumerate((fd, fx, fy, f)):
        wrows = pl.ds(pl.multiple_of(dest * cols, cols), cols)
        for i in range(2):
            rows = slice(i * mrows, (i + 1) * mrows)
            live = live_of(i)
            full = grad[rows, wrows] + live * product(1, rows, wrows)
            full = (live * full).astype(jnp.bfloat16)
            full = full.reshape(mrows // BLK, BLK, cols)
            spots = pl.ds(i * (mrows // BLK), mrows // BLK)
            if n < 3:
                rg[n, spots] = full
            else:
                gcols[pl.ds(f * (seq // BLK) + i * (mrows // BLK), mrows // BLK)] = full
        if n < 3:
            copy = pltpu.make_async_remote_copy(
                src_ref=rg.at[n],
                dst_ref=gcols.at[pl.ds(f * (seq // BLK), seq // BLK)],
                send_sem=feat_s.at[n],
                recv_sem=feat_r.at[n],
                device_id=(dest, g),
                device_id_type=MESH,
            )
            copy.start()
            feat_copies.append(copy)
    for copy in feat_copies:
        copy.wait()

    order = [m for m in range(owner_count - 1, 0, -1)]
    order = sorted(order, key=lambda m: -(m // 2))
    row_copies = []
    for m in order:
        dest = flip(g, m)

        def pick(s, c, dest=dest, m=m):
            src = src_ref[dest * slot_cap + s]
            send[m, s] = gcols[src]
            return c

        lax.fori_loop(0, slot_cap, pick, 0, unroll=True)
        copy = pltpu.make_async_remote_copy(
            src_ref=send.at[m],
            dst_ref=rows_out.at[g],
            send_sem=row_s.at[m - 1],
            recv_sem=row_r.at[m - 1],
            device_id=(f, dest),
            device_id_type=MESH,
        )
        copy.start()
        row_copies.append(copy)

    def pick_own(s, c):
        src = src_ref[g * slot_cap + s]
        rows_out[g, s] = gcols[src]
        return c

    lax.fori_loop(0, slot_cap, pick_own, 0, unroll=True)
    for copy in id_copies + row_copies:
        copy.wait()
    for l in range(2):
        for w in range(2):
            for s in range(2):
                directs[l][w][s].wait_send()
        for s in range(2):
            relays[l][s].wait_send()
        for i in range(3):
            forwards[l][i].wait_send()


def table_kernel(ids_ref, rows_ref, out_ref, wide, *tables):
    slots = ids_ref.shape[0]
    chunk = out_ref.shape[1]

    @pl.when(pl.program_id(0) == 0)
    def _():
        def clear(i, c):
            spot = pl.ds(pl.multiple_of(i * 128, 128), 128)
            for table in tables:
                table[spot, :] = jnp.zeros((128, table.shape[1]), jnp.float32)
            return c

        lax.fori_loop(0, ROWS_OWN // 128, clear, 0)

        def add_slot(s, c):
            @pl.when(ids_ref[s, 0] >= 0)
            def _():
                base = pl.multiple_of(s * BLK, BLK)
                wide[...] = rows_ref[pl.ds(base, BLK), :].astype(jnp.float32)
                for r in range(0, BLK, TABLES):
                    spots = [pl.ds(ids_ref[s, r + q], 1) for q in range(TABLES)]
                    olds = [tables[q][spots[q], :] for q in range(TABLES)]
                    for q in range(TABLES):
                        tables[q][spots[q], :] = olds[q] + wide[r + q : r + q + 1, :]

            return c

        lax.fori_loop(0, slots, add_slot, 0)

    spot = pl.ds(pl.multiple_of(pl.program_id(0) * chunk, chunk), chunk)
    total = tables[0][spot, :]
    for table in tables[1:]:
        total = total + table[spot, :]
    out_ref[...] = total.T


def fused_body(grad_out, pre_first, pre_second, conv_first, conv_second, lengths, item_ids, owners):
    seq, width = grad_out.shape[1:]
    cols = conv_first.shape[1]
    owner_count = lax.axis_size("grp")
    blocks = owners.shape[0]
    slot_cap = max(2, 2 * blocks // owner_count)
    slots = owner_count * slot_cap
    smem = pl.BlockSpec(memory_space=pltpu.SMEM)
    vmem = pl.BlockSpec(memory_space=pltpu.VMEM)
    source, send_ids = pl.pallas_call(
        functools.partial(plan_kernel, slot_cap),
        out_shape=(
            jax.ShapeDtypeStruct((slots,), jnp.int32),
            jax.ShapeDtypeStruct((slots, BLK), jnp.int32),
        ),
        in_specs=[smem, vmem],
        out_specs=(smem, vmem),
        scratch_shapes=[pltpu.SMEM((owner_count,), jnp.int32)],
    )(owners.reshape(blocks), item_ids.reshape(blocks, BLK))
    dma = pltpu.SemaphoreType.DMA
    bf16 = jnp.bfloat16
    rows, ids = pl.pallas_call(
        functools.partial(exchange_kernel, slot_cap, owner_count),
        out_shape=(
            jax.ShapeDtypeStruct((owner_count, slot_cap, BLK, cols), bf16),
            jax.ShapeDtypeStruct((slots, BLK), jnp.int32),
        ),
        in_specs=[smem, smem] + [vmem] * 6,
        out_specs=(vmem, vmem),
        scratch_shapes=[
            pltpu.VMEM((2, 3, width, width), bf16),
            pltpu.VMEM((seq + 2 * PAD, width), jnp.float32),
            pltpu.VMEM((3, seq, width), bf16),
            pltpu.VMEM((seq, width), jnp.float32),
            pltpu.VMEM((3, seq // BLK, BLK, cols), bf16),
            pltpu.VMEM((4 * seq // BLK, BLK, cols), bf16),
            pltpu.VMEM((owner_count, slot_cap, BLK, cols), bf16),
            dma((2, 2, 2)),
            dma((2, 2, 2)),
            dma((2, 2)),
            dma((2, 2)),
            dma((2, 3)),
            dma((2, 3)),
            dma((3,)),
            dma((3,)),
            dma((owner_count - 1,)),
            dma((owner_count - 1,)),
            dma((owner_count - 1,)),
            dma((owner_count - 1,)),
        ],
        compiler_params=pltpu.CompilerParams(collective_id=0, has_side_effects=True),
    )(
        source,
        lengths,
        send_ids,
        grad_out.reshape(seq, width),
        pre_first.reshape(seq, width),
        pre_second.reshape(seq, width),
        conv_first,
        conv_second,
    )
    chunk = 512
    return pl.pallas_call(
        table_kernel,
        grid=(ROWS_OWN // chunk,),
        out_shape=jax.ShapeDtypeStruct((cols, ROWS_OWN), jnp.float32),
        in_specs=[smem, pl.BlockSpec((slots * BLK, cols), lambda i: (0, 0))],
        out_specs=pl.BlockSpec((cols, chunk), lambda i: (0, i)),
        scratch_shapes=[pltpu.VMEM((BLK, cols), jnp.float32)]
        + [pltpu.VMEM((ROWS_OWN, cols), jnp.float32)] * TABLES,
    )(ids, rows.reshape(slots * BLK, cols))


def layer_back(gradient, pre_acts, live_rows, dilation, product):
    seq_len = gradient.shape[0]
    pre_float = pre_acts.astype(jnp.float32)
    sig_val = jax.nn.sigmoid(pre_float)
    deltas = (gradient * sig_val * (1.0 + pre_float * (1.0 - sig_val))).astype(jnp.bfloat16)
    padded = jnp.pad(deltas, ((dilation, dilation), (0, 0)))
    tap_rows = jnp.stack(
        [
            padded[2 * dilation : 2 * dilation + seq_len],
            padded[dilation : dilation + seq_len],
            padded[0:seq_len],
        ]
    )
    return gradient + live_rows * product(tap_rows)


def gathered_product(weights):

    def apply_taps(tap_rows):
        return jnp.einsum(
            "ktd,kpd->tp",
            tap_rows,
            lax.all_gather(weights, "fsdp", axis=1, tiled=True),
            preferred_element_type=jnp.float32,
        )

    return apply_taps


def body(grad_out, pre_first, pre_second, conv_first, conv_second, lengths, item_ids, owners):
    seq_len = grad_out.shape[1]
    positions = jnp.arange(seq_len, dtype=jnp.int32)
    live_rows = (positions < lengths[0]).astype(jnp.float32)[:, None]
    gradient = grad_out[0].astype(jnp.float32)
    gradient = layer_back(gradient, pre_second[0], live_rows, 2, gathered_product(conv_second))
    gradient = layer_back(gradient, pre_first[0], live_rows, 1, gathered_product(conv_first))
    row_grad = (live_rows * gradient).astype(jnp.bfloat16)
    group_cols = lax.all_to_all(row_grad.T, "fsdp", split_axis=0, concat_axis=1, tiled=True)
    feat_cols = group_cols.shape[0]
    owner_count = lax.axis_size("grp")
    blocks = owners.shape[0]
    slot_cap = max(2, 2 * blocks // owner_count)
    block_dest = owners[:, 0]
    dest_hits = (block_dest[:, None] == jnp.arange(owner_count, dtype=jnp.int32)[None, :]).astype(
        jnp.int32
    )
    earlier = jnp.cumsum(dest_hits, axis=0) - dest_hits
    block_rank = jnp.sum(dest_hits * earlier, axis=1)
    slot_index = block_dest * slot_cap + block_rank
    select_int = (
        slot_index[:, None] == jnp.arange(owner_count * slot_cap, dtype=jnp.int32)[None, :]
    ).astype(jnp.int32)
    select_int = select_int.reshape(blocks, owner_count, slot_cap)
    select_map = select_int.astype(jnp.bfloat16)
    block_cols = group_cols.reshape(feat_cols, blocks, BLK)
    send_rows = jnp.einsum(
        "cbr,bos->ocsr", block_cols, select_map, preferred_element_type=jnp.float32
    )
    send_rows = send_rows.astype(jnp.bfloat16).reshape(owner_count, feat_cols, slot_cap * BLK)
    shifted_ids = item_ids.reshape(blocks, BLK) + 1
    send_ids = jnp.einsum("br,bos->osr", shifted_ids, select_int) - 1
    send_ids = send_ids.reshape(owner_count, slot_cap * BLK)
    recv_rows, recv_ids = (
        lax.all_to_all(send_rows, "grp", split_axis=0, concat_axis=0, tiled=True),
        lax.all_to_all(send_ids, "grp", split_axis=0, concat_axis=0, tiled=True),
    )
    flat_rows = jnp.transpose(recv_rows, (0, 2, 1)).reshape(-1, feat_cols).astype(jnp.float32)
    safe_ids = jnp.where(recv_ids < 0, ROWS_OWN, recv_ids).reshape(-1)
    summed = jax.ops.segment_sum(flat_rows, safe_ids, num_segments=ROWS_OWN + 1)
    return summed[:ROWS_OWN].T


def solution(mesh):
    fused = mesh.shape["fsdp"] == 4 and mesh.shape["grp"] == 8
    placed = (
        P(("fsdp", "grp"), None, None),
        P(("fsdp", "grp"), None, None),
        P(("fsdp", "grp"), None, None),
        P(None, "fsdp", None),
        P(None, "fsdp", None),
        P(("fsdp", "grp")),
        P("grp"),
        P("grp", None),
    )
    return jax.shard_map(
        fused_body if fused else body, mesh=mesh, in_specs=placed, out_specs=P("fsdp", "grp"), check_vma=False
    )
```

```python
import functools

import jax
import jax.numpy as jnp
from jax import lax
from jax.experimental import pallas as pl
from jax.experimental.pallas import tpu as pltpu
from jax.sharding import PartitionSpec as P

MESH = pl.DeviceIdType.MESH
BLK = 32
ROWS_OWN = 8192
PAD = 8
TABLES = 4


def flip(index, mask):
    out = 0
    for bit in range(6):
        have = (index // (1 << bit)) % 2
        out = out + ((1 - have) if (mask >> bit) & 1 else have) * (1 << bit)
    return out


def slot_plan(slot_cap, slots, own_row, ids_ref):
    blocks = own_row.shape[1]
    early = lax.broadcasted_iota(jnp.int32, (blocks, blocks), 0)
    late = lax.broadcasted_iota(jnp.int32, (blocks, blocks), 1)
    own_late = jnp.broadcast_to(own_row, (blocks, blocks))
    own_early = jnp.sum(jnp.where(early == late, own_late, 0), axis=1, keepdims=True)
    same = (own_early == own_late) & (early < late)
    rank = jnp.sum(jnp.where(same, 1, 0), axis=0, keepdims=True)
    slot = own_row * slot_cap + rank
    hit = slot == lax.broadcasted_iota(jnp.int32, (slots, blocks), 0)
    index = lax.broadcasted_iota(jnp.int32, (slots, blocks), 1)
    source = jnp.sum(jnp.where(hit, index, 0), axis=1, keepdims=True)
    used = jnp.sum(jnp.where(hit, 1, 0), axis=1, keepdims=True)
    lanes = ids_ref.shape[1]
    row_of = jnp.broadcast_to(source >> 2, (slots, lanes))
    lane_of = jnp.broadcast_to(source & 3, (slots, lanes))
    used = jnp.broadcast_to(used, (slots, lanes))
    ids = jnp.zeros((slots, lanes), jnp.int32)
    for r in range(ids_ref.shape[0]):
        ids = jnp.where(row_of == r, ids_ref[r : r + 1, :], ids)
    out = ids
    for q in range(1, 4):
        out = jnp.where(lane_of == q, pltpu.roll(ids, lanes - q * BLK, 1), out)
    return jnp.broadcast_to(source, (slots, lanes)), jnp.where(used > 0, out, -1)


def exchange_kernel(
    slot_cap,
    owner_count,
    len_ref,
    own_ref,
    item_ref,
    go_ref,
    p1_ref,
    p2_ref,
    w1_ref,
    w2_ref,
    rows_out,
    ids_out,
    wfull,
    pad,
    dsh,
    grad,
    rg,
    gcols,
    send,
    dir_s,
    dir_r,
    rel_s,
    rel_r,
    fw_s,
    fw_r,
    feat_s,
    feat_r,
    row_s,
    row_r,
    id_s,
    id_r,
    ids_ref,
    src_vmem,
    src_ref,
    src_sem,
):
    f = lax.axis_index("fsdp")
    g = lax.axis_index("grp")
    core = g % 2
    seq = grad.shape[0]
    width = grad.shape[1]
    cols = width // 4
    half = cols // 2
    quarter = cols // 4
    fx, fy, fd = flip(f, 1), flip(f, 2), flip(f, 3)
    mate = flip(g, 1)

    barrier = pltpu.get_barrier_semaphore()
    for peer in (fx, fy, fd):
        pl.semaphore_signal(barrier, inc=1, device_id=(peer, g), device_id_type=MESH)
    for m in range(1, owner_count):
        pl.semaphore_signal(barrier, inc=1, device_id=(f, flip(g, m)), device_id_type=MESH)
    pad[0:PAD, :] = jnp.zeros((PAD, width), jnp.float32)
    pad[PAD + seq : 2 * PAD + seq, :] = jnp.zeros((PAD, width), jnp.float32)
    own_cols = pl.ds(pl.multiple_of(f * cols, cols), cols)
    wfull[0, :, own_cols, :] = w2_ref[...]
    wfull[1, :, own_cols, :] = w1_ref[...]
    pl.semaphore_wait(barrier, 3 + owner_count - 1)

    w_refs = (w2_ref, w1_ref)

    def part(layer, owner, off, rows):
        return wfull.at[layer, :, pl.ds(pl.multiple_of(owner * cols + off, quarter), rows), :]

    def direct(layer, way, sub):
        peer = (fx, fy)[way]
        off = core * half + sub * quarter
        return pltpu.make_async_remote_copy(
            src_ref=w_refs[layer].at[:, pl.ds(pl.multiple_of(off, quarter), quarter), :],
            dst_ref=part(layer, f, off, quarter),
            send_sem=dir_s.at[layer, way, sub],
            recv_sem=dir_r.at[layer, way, sub],
            device_id=(peer, g),
            device_id_type=MESH,
        )

    def relay(layer, sub):
        holder, peer = ((fx, fy), (fy, fx))[sub]
        place = part(layer, holder, core * half + sub * quarter, quarter)
        return pltpu.make_async_remote_copy(
            src_ref=place,
            dst_ref=place,
            send_sem=rel_s.at[layer, sub],
            recv_sem=rel_r.at[layer, sub],
            device_id=(peer, g),
            device_id_type=MESH,
        )

    def forward(layer, which):
        place = part(layer, (fx, fy, fd)[which], core * half, half)
        return pltpu.make_async_remote_copy(
            src_ref=place,
            dst_ref=place,
            send_sem=fw_s.at[layer, which],
            recv_sem=fw_r.at[layer, which],
            device_id=(f, mate),
            device_id_type=MESH,
        )

    directs = [[[direct(l, w, s) for s in range(2)] for w in range(2)] for l in range(2)]
    relays = [[relay(l, s) for s in range(2)] for l in range(2)]
    forwards = [[forward(l, i) for i in range(3)] for l in range(2)]

    def start_directs(layer):
        directs[layer][0][0].start()
        directs[layer][1][1].start()
        directs[layer][0][1].start()
        directs[layer][1][0].start()

    def start_relays(layer):
        directs[layer][0][0].wait_recv()
        relays[layer][0].start()
        directs[layer][1][1].wait_recv()
        relays[layer][1].start()

    def start_near_forwards(layer):
        directs[layer][0][1].wait_recv()
        forwards[layer][0].start()
        directs[layer][1][0].wait_recv()
        forwards[layer][1].start()

    def start_far_forward(layer):
        relays[layer][0].wait_recv()
        relays[layer][1].wait_recv()
        forwards[layer][2].start()

    start_directs(0)
    source, send_ids = slot_plan(slot_cap, owner_count * slot_cap, own_ref[...], item_ref)
    ids_ref[...] = send_ids
    src_vmem[...] = source
    src_copy = pltpu.make_async_copy(src_vmem, src_ref, src_sem)
    src_copy.start()

    id_copies = []
    for m in range(1, owner_count):
        dest = flip(g, m)
        id_copies.append(
            pltpu.make_async_remote_copy(
                src_ref=ids_ref.at[pl.ds(pl.multiple_of(dest * slot_cap, slot_cap), slot_cap), :],
                dst_ref=ids_out.at[pl.ds(pl.multiple_of(g * slot_cap, slot_cap), slot_cap), :],
                send_sem=id_s.at[m - 1],
                recv_sem=id_r.at[m - 1],
                device_id=(f, dest),
                device_id_type=MESH,
            )
        )
        id_copies[-1].start()
    own_ids = pl.ds(pl.multiple_of(g * slot_cap, slot_cap), slot_cap)
    ids_out[own_ids, :] = ids_ref[own_ids, :]

    step = 64

    def taps(first, pre_ref, dilation):
        for i in range(seq // step):
            rows = slice(i * step, (i + 1) * step)
            z = pre_ref[rows, :].astype(jnp.float32)
            s = jax.nn.sigmoid(z)
            grad_rows = first[rows, :].astype(jnp.float32)
            d = (grad_rows * s * (1.0 + z * (1.0 - s))).astype(jnp.bfloat16)
            dsh[1, rows, :] = d
            pad[PAD + i * step : PAD + (i + 1) * step, :] = d.astype(jnp.float32)
        for i in range(seq // step):
            rows = slice(i * step, (i + 1) * step)
            low = PAD + i * step
            dsh[0, rows, :] = pad[low + dilation : low + dilation + step, :].astype(jnp.bfloat16)
            dsh[2, rows, :] = pad[low - dilation : low - dilation + step, :].astype(jnp.bfloat16)

    def product(layer, rows, wrows):
        total = None
        for k in range(3):
            one = lax.dot_general(
                dsh[k, rows, :],
                wfull[layer, k, wrows, :],
                (((1,), (1,)), ((), ())),
                preferred_element_type=jnp.float32,
            )
            total = one if total is None else total + one
        return total

    mrows = seq // 2

    def live_of(i):
        spots = lax.broadcasted_iota(jnp.int32, (mrows, 1), 0) + i * mrows
        return (spots < len_ref[0]).astype(jnp.float32)

    taps(go_ref, p2_ref, 2)
    start_relays(0)
    start_directs(1)
    start_near_forwards(0)
    for n, dest in enumerate((f, fx, fy, fd)):
        if n == 2:
            start_far_forward(0)
        if n > 0:
            forwards[0][n - 1].wait_recv()
        if n == 3:
            start_relays(1)
        wrows = pl.ds(pl.multiple_of(dest * cols, cols), cols)
        for i in range(2):
            rows = slice(i * mrows, (i + 1) * mrows)
            grad[rows, wrows] = go_ref[rows, wrows].astype(jnp.float32) + live_of(i) * product(
                0, rows, wrows
            )
    taps(grad, p1_ref, 1)
    start_near_forwards(1)

    feat_copies = []
    for n, dest in enumerate((f, fx, fy, fd)):
        if n == 2:
            start_far_forward(1)
        if n > 0:
            forwards[1][n - 1].wait_recv()
        wrows = pl.ds(pl.multiple_of(dest * cols, cols), cols)
        for i in range(2):
            rows = slice(i * mrows, (i + 1) * mrows)
            live = live_of(i)
            full = grad[rows, wrows] + live * product(1, rows, wrows)
            full = (live * full).astype(jnp.bfloat16)
            full = full.reshape(mrows // BLK, BLK, cols)
            spots = pl.ds(i * (mrows // BLK), mrows // BLK)
            if n > 0:
                rg[n - 1, spots] = full
            else:
                gcols[pl.ds(f * (seq // BLK) + i * (mrows // BLK), mrows // BLK)] = full
        if n > 0:
            copy = pltpu.make_async_remote_copy(
                src_ref=rg.at[n - 1],
                dst_ref=gcols.at[pl.ds(f * (seq // BLK), seq // BLK)],
                send_sem=feat_s.at[n - 1],
                recv_sem=feat_r.at[n - 1],
                device_id=(dest, g),
                device_id_type=MESH,
            )
            copy.start()
            feat_copies.append(copy)
    src_copy.wait()
    for copy in feat_copies:
        copy.wait()

    order = [m for m in range(owner_count - 1, 0, -1)]
    order = sorted(order, key=lambda m: -(m // 2))
    row_copies = []
    for m in order:
        dest = flip(g, m)

        def pick(s, c, dest=dest, m=m):
            src = src_ref[dest * slot_cap + s, 0]
            send[m, s] = gcols[src]
            return c

        lax.fori_loop(0, slot_cap, pick, 0, unroll=True)
        copy = pltpu.make_async_remote_copy(
            src_ref=send.at[m],
            dst_ref=rows_out.at[g],
            send_sem=row_s.at[m - 1],
            recv_sem=row_r.at[m - 1],
            device_id=(f, dest),
            device_id_type=MESH,
        )
        copy.start()
        row_copies.append(copy)

    def pick_own(s, c):
        src = src_ref[g * slot_cap + s, 0]
        rows_out[g, s] = gcols[src]
        return c

    lax.fori_loop(0, slot_cap, pick_own, 0, unroll=True)
    for copy in id_copies + row_copies:
        copy.wait()
    for l in range(2):
        for w in range(2):
            for s in range(2):
                directs[l][w][s].wait_send()
        for s in range(2):
            relays[l][s].wait_send()
        for i in range(3):
            forwards[l][i].wait_send()


def table_kernel(ids_ref, rows_ref, out_ref, wide, *tables):
    slots = ids_ref.shape[0]
    chunk = out_ref.shape[1]

    @pl.when(pl.program_id(0) == 0)
    def _():
        def clear(i, c):
            spot = pl.ds(pl.multiple_of(i * 128, 128), 128)
            for table in tables:
                table[spot, :] = jnp.zeros((128, table.shape[1]), jnp.float32)
            return c

        lax.fori_loop(0, ROWS_OWN // 128, clear, 0)

        def add_slot(s, c):
            @pl.when(ids_ref[s, 0] >= 0)
            def _():
                base = pl.multiple_of(s * BLK, BLK)
                wide[...] = rows_ref[pl.ds(base, BLK), :].astype(jnp.float32)
                for r in range(0, BLK, TABLES):
                    spots = [pl.ds(ids_ref[s, r + q], 1) for q in range(TABLES)]
                    olds = [tables[q][spots[q], :] for q in range(TABLES)]
                    for q in range(TABLES):
                        tables[q][spots[q], :] = olds[q] + wide[r + q : r + q + 1, :]

            return c

        lax.fori_loop(0, slots, add_slot, 0)

    spot = pl.ds(pl.multiple_of(pl.program_id(0) * chunk, chunk), chunk)
    total = tables[0][spot, :]
    for table in tables[1:]:
        total = total + table[spot, :]
    out_ref[...] = total.T


def fused_body(grad_out, pre_first, pre_second, conv_first, conv_second, lengths, item_ids, owners):
    seq, width = grad_out.shape[1:]
    cols = conv_first.shape[1]
    owner_count = lax.axis_size("grp")
    blocks = owners.shape[0]
    slot_cap = max(2, 2 * blocks // owner_count)
    slots = owner_count * slot_cap
    smem = pl.BlockSpec(memory_space=pltpu.SMEM)
    vmem = pl.BlockSpec(memory_space=pltpu.VMEM)
    dma = pltpu.SemaphoreType.DMA
    bf16 = jnp.bfloat16
    rows, ids = pl.pallas_call(
        functools.partial(exchange_kernel, slot_cap, owner_count),
        out_shape=(
            jax.ShapeDtypeStruct((owner_count, slot_cap, BLK, cols), bf16),
            jax.ShapeDtypeStruct((slots, 4 * BLK), jnp.int32),
        ),
        in_specs=[smem] + [vmem] * 7,
        out_specs=(vmem, vmem),
        scratch_shapes=[
            pltpu.VMEM((2, 3, width, width), bf16),
            pltpu.VMEM((seq + 2 * PAD, width), jnp.float32),
            pltpu.VMEM((3, seq, width), bf16),
            pltpu.VMEM((seq, width), jnp.float32),
            pltpu.VMEM((3, seq // BLK, BLK, cols), bf16),
            pltpu.VMEM((4 * seq // BLK, BLK, cols), bf16),
            pltpu.VMEM((owner_count, slot_cap, BLK, cols), bf16),
            dma((2, 2, 2)),
            dma((2, 2, 2)),
            dma((2, 2)),
            dma((2, 2)),
            dma((2, 3)),
            dma((2, 3)),
            dma((3,)),
            dma((3,)),
            dma((owner_count - 1,)),
            dma((owner_count - 1,)),
            dma((owner_count - 1,)),
            dma((owner_count - 1,)),
            pltpu.VMEM((slots, 4 * BLK), jnp.int32),
            pltpu.VMEM((slots, 4 * BLK), jnp.int32),
            pltpu.SMEM((slots, 4 * BLK), jnp.int32),
            dma,
        ],
        compiler_params=pltpu.CompilerParams(collective_id=0, has_side_effects=True),
    )(
        lengths,
        owners.reshape(1, blocks),
        item_ids.reshape(blocks // 4, 4 * BLK),
        grad_out.reshape(seq, width),
        pre_first.reshape(seq, width),
        pre_second.reshape(seq, width),
        conv_first,
        conv_second,
    )
    chunk = 4096
    return pl.pallas_call(
        table_kernel,
        grid=(ROWS_OWN // chunk,),
        out_shape=jax.ShapeDtypeStruct((cols, ROWS_OWN), jnp.float32),
        in_specs=[smem, pl.BlockSpec((slots * BLK, cols), lambda i: (0, 0))],
        out_specs=pl.BlockSpec((cols, chunk), lambda i: (0, i)),
        scratch_shapes=[pltpu.VMEM((BLK, cols), jnp.float32)]
        + [pltpu.VMEM((ROWS_OWN, cols), jnp.float32)] * TABLES,
    )(ids, rows.reshape(slots * BLK, cols))


def layer_back(gradient, pre_acts, live_rows, dilation, product):
    seq_len = gradient.shape[0]
    pre_float = pre_acts.astype(jnp.float32)
    sig_val = jax.nn.sigmoid(pre_float)
    deltas = (gradient * sig_val * (1.0 + pre_float * (1.0 - sig_val))).astype(jnp.bfloat16)
    padded = jnp.pad(deltas, ((dilation, dilation), (0, 0)))
    tap_rows = jnp.stack(
        [
            padded[2 * dilation : 2 * dilation + seq_len],
            padded[dilation : dilation + seq_len],
            padded[0:seq_len],
        ]
    )
    return gradient + live_rows * product(tap_rows)


def gathered_product(weights):

    def apply_taps(tap_rows):
        return jnp.einsum(
            "ktd,kpd->tp",
            tap_rows,
            lax.all_gather(weights, "fsdp", axis=1, tiled=True),
            preferred_element_type=jnp.float32,
        )

    return apply_taps


def body(grad_out, pre_first, pre_second, conv_first, conv_second, lengths, item_ids, owners):
    seq_len = grad_out.shape[1]
    positions = jnp.arange(seq_len, dtype=jnp.int32)
    live_rows = (positions < lengths[0]).astype(jnp.float32)[:, None]
    gradient = grad_out[0].astype(jnp.float32)
    gradient = layer_back(gradient, pre_second[0], live_rows, 2, gathered_product(conv_second))
    gradient = layer_back(gradient, pre_first[0], live_rows, 1, gathered_product(conv_first))
    row_grad = (live_rows * gradient).astype(jnp.bfloat16)
    group_cols = lax.all_to_all(row_grad.T, "fsdp", split_axis=0, concat_axis=1, tiled=True)
    feat_cols = group_cols.shape[0]
    owner_count = lax.axis_size("grp")
    blocks = owners.shape[0]
    slot_cap = max(2, 2 * blocks // owner_count)
    block_dest = owners[:, 0]
    dest_hits = (block_dest[:, None] == jnp.arange(owner_count, dtype=jnp.int32)[None, :]).astype(
        jnp.int32
    )
    earlier = jnp.cumsum(dest_hits, axis=0) - dest_hits
    block_rank = jnp.sum(dest_hits * earlier, axis=1)
    slot_index = block_dest * slot_cap + block_rank
    select_int = (
        slot_index[:, None] == jnp.arange(owner_count * slot_cap, dtype=jnp.int32)[None, :]
    ).astype(jnp.int32)
    select_int = select_int.reshape(blocks, owner_count, slot_cap)
    select_map = select_int.astype(jnp.bfloat16)
    block_cols = group_cols.reshape(feat_cols, blocks, BLK)
    send_rows = jnp.einsum(
        "cbr,bos->ocsr", block_cols, select_map, preferred_element_type=jnp.float32
    )
    send_rows = send_rows.astype(jnp.bfloat16).reshape(owner_count, feat_cols, slot_cap * BLK)
    shifted_ids = item_ids.reshape(blocks, BLK) + 1
    send_ids = jnp.einsum("br,bos->osr", shifted_ids, select_int) - 1
    send_ids = send_ids.reshape(owner_count, slot_cap * BLK)
    recv_rows, recv_ids = (
        lax.all_to_all(send_rows, "grp", split_axis=0, concat_axis=0, tiled=True),
        lax.all_to_all(send_ids, "grp", split_axis=0, concat_axis=0, tiled=True),
    )
    flat_rows = jnp.transpose(recv_rows, (0, 2, 1)).reshape(-1, feat_cols).astype(jnp.float32)
    safe_ids = jnp.where(recv_ids < 0, ROWS_OWN, recv_ids).reshape(-1)
    summed = jax.ops.segment_sum(flat_rows, safe_ids, num_segments=ROWS_OWN + 1)
    return summed[:ROWS_OWN].T


def solution(mesh):
    fused = mesh.shape["fsdp"] == 4 and mesh.shape["grp"] == 8
    placed = (
        P(("fsdp", "grp"), None, None),
        P(("fsdp", "grp"), None, None),
        P(("fsdp", "grp"), None, None),
        P(None, "fsdp", None),
        P(None, "fsdp", None),
        P(("fsdp", "grp")),
        P("grp"),
        P("grp", None),
    )
    return jax.shard_map(
        fused_body if fused else body, mesh=mesh, in_specs=placed, out_specs=P("fsdp", "grp"), check_vma=False
    )
```

```python
import functools

import jax
import jax.numpy as jnp
from jax import lax
from jax.experimental import pallas as pl
from jax.experimental.pallas import tpu as pltpu
from jax.sharding import PartitionSpec as P

MESH = pl.DeviceIdType.MESH
BLK = 32
ROWS_OWN = 8192
PAD = 8
TABLES = 4


def flip(index, mask):
    out = 0
    for bit in range(6):
        have = (index // (1 << bit)) % 2
        out = out + ((1 - have) if (mask >> bit) & 1 else have) * (1 << bit)
    return out


def slot_plan(slot_cap, slots, own_row, ids_ref):
    blocks = own_row.shape[1]
    early = lax.broadcasted_iota(jnp.int32, (blocks, blocks), 0)
    late = lax.broadcasted_iota(jnp.int32, (blocks, blocks), 1)
    own_late = jnp.broadcast_to(own_row, (blocks, blocks))
    own_early = jnp.sum(jnp.where(early == late, own_late, 0), axis=1, keepdims=True)
    same = (own_early == own_late) & (early < late)
    rank = jnp.sum(jnp.where(same, 1, 0), axis=0, keepdims=True)
    slot = own_row * slot_cap + rank
    hit = slot == lax.broadcasted_iota(jnp.int32, (slots, blocks), 0)
    index = lax.broadcasted_iota(jnp.int32, (slots, blocks), 1)
    source = jnp.sum(jnp.where(hit, index, 0), axis=1, keepdims=True)
    used = jnp.sum(jnp.where(hit, 1, 0), axis=1, keepdims=True)
    lanes = ids_ref.shape[1]
    row_of = jnp.broadcast_to(source >> 2, (slots, lanes))
    lane_of = jnp.broadcast_to(source & 3, (slots, lanes))
    used = jnp.broadcast_to(used, (slots, lanes))
    ids = jnp.zeros((slots, lanes), jnp.int32)
    for r in range(ids_ref.shape[0]):
        ids = jnp.where(row_of == r, ids_ref[r : r + 1, :], ids)
    out = ids
    for q in range(1, 4):
        out = jnp.where(lane_of == q, pltpu.roll(ids, lanes - q * BLK, 1), out)
    return jnp.broadcast_to(source, (slots, lanes)), jnp.where(used > 0, out, -1)


def exchange_kernel(
    slot_cap,
    owner_count,
    len_ref,
    own_ref,
    item_ref,
    go_ref,
    p1_ref,
    p2_ref,
    w1_ref,
    w2_ref,
    rows_out,
    ids_out,
    wfull,
    pad,
    dsh,
    grad,
    rg,
    gcols,
    send,
    dir_s,
    dir_r,
    rel_s,
    rel_r,
    up_s,
    up_r,
    fw_s,
    fw_r,
    feat_s,
    feat_r,
    row_s,
    row_r,
    id_s,
    id_r,
    ids_ref,
    src_vmem,
    src_ref,
    src_sem,
):
    f = lax.axis_index("fsdp")
    g = lax.axis_index("grp")
    core = g % 2
    seq = grad.shape[0]
    width = grad.shape[1]
    cols = width // 4
    half = cols // 2
    quarter = cols // 4
    fx, fy, fd = flip(f, 1), flip(f, 2), flip(f, 3)
    mate = flip(g, 1)
    level = flip(g, 2)
    first_tap = 1 + (g // 2) % 2
    tap_of = (first_tap, 0, 3 - first_tap)

    barrier = pltpu.get_barrier_semaphore()
    for peer in (fx, fy, fd):
        pl.semaphore_signal(barrier, inc=1, device_id=(peer, g), device_id_type=MESH)
    for m in range(1, owner_count):
        pl.semaphore_signal(barrier, inc=1, device_id=(f, flip(g, m)), device_id_type=MESH)
    pad[0:PAD, :] = jnp.zeros((PAD, width), jnp.float32)
    pad[PAD + seq : 2 * PAD + seq, :] = jnp.zeros((PAD, width), jnp.float32)
    own_cols = pl.ds(pl.multiple_of(f * cols, cols), cols)
    wfull[0, :, own_cols, :] = w2_ref[...]
    wfull[1, :, own_cols, :] = w1_ref[...]
    pl.semaphore_wait(barrier, 3 + owner_count - 1)

    w_refs = (w2_ref, w1_ref)

    def part(layer, turn, owner, off, rows):
        spot = pl.ds(pl.multiple_of(owner * cols + off, quarter), rows)
        return wfull.at[layer, tap_of[turn], spot, :]

    def move(src, dst, send_sem, recv_sem, peer):
        return pltpu.make_async_remote_copy(
            src_ref=src,
            dst_ref=dst,
            send_sem=send_sem,
            recv_sem=recv_sem,
            device_id=peer,
            device_id_type=MESH,
        )

    def direct(layer, turn, way, sub):
        off = core * half + sub * quarter
        spot = pl.ds(pl.multiple_of(off, quarter), quarter)
        at = (layer, turn, way, sub)
        return move(
            w_refs[layer].at[tap_of[turn], spot, :],
            part(layer, turn, f, off, quarter),
            dir_s.at[at],
            dir_r.at[at],
            ((fx, fy)[way], g),
        )

    def relay(layer, turn, sub):
        holder, peer = ((fx, fy), (fy, fx))[sub]
        place = part(layer, turn, holder, core * half + sub * quarter, quarter)
        at = (layer, turn, sub)
        return move(place, place, rel_s.at[at], rel_r.at[at], (peer, g))

    def along(layer, which):
        place = part(layer, 0, (fx, fy, fd)[which], core * half, half)
        at = (layer, which)
        return move(place, place, up_s.at[at], up_r.at[at], (f, level))

    def forward(layer, turn, which):
        place = part(layer, turn, (fx, fy, fd)[which], core * half, half)
        at = (layer, turn, which)
        return move(place, place, fw_s.at[at], fw_r.at[at], (f, mate))

    two, three = range(2), range(3)
    directs = [[[[direct(l, t, w, s) for s in two] for w in two] for t in two] for l in two]
    relays = [[[relay(l, t, s) for s in two] for t in two] for l in two]
    alongs = [[along(l, i) for i in three] for l in two]
    forwards = [[[forward(l, t, i) for i in three] for t in three] for l in two]

    def start_directs(layer):
        for turn in two:
            directs[layer][turn][0][0].start()
            directs[layer][turn][1][1].start()
            directs[layer][turn][0][1].start()
            directs[layer][turn][1][0].start()

    def near(layer, turn):
        directs[layer][turn][0][0].wait_recv()
        relays[layer][turn][0].start()
        directs[layer][turn][1][1].wait_recv()
        relays[layer][turn][1].start()
        for way in two:
            directs[layer][turn][way][1 - way].wait_recv()
            if turn == 0:
                alongs[layer][way].start()
            forwards[layer][turn][way].start()

    def far(layer):
        for turn in two:
            relays[layer][turn][0].wait_recv()
            relays[layer][turn][1].wait_recv()
            if turn == 0:
                alongs[layer][2].start()
            forwards[layer][turn][2].start()

    def upper(layer):
        for which in three:
            alongs[layer][which].wait_recv()
            forwards[layer][2][which].start()

    def shard_ready(layer, which):
        for turn in three:
            forwards[layer][turn][which].wait_recv()

    start_directs(0)
    source, send_ids = slot_plan(slot_cap, owner_count * slot_cap, own_ref[...], item_ref)
    ids_ref[...] = send_ids
    src_vmem[...] = source
    src_copy = pltpu.make_async_copy(src_vmem, src_ref, src_sem)
    src_copy.start()

    id_copies = []
    for m in range(1, owner_count):
        dest = flip(g, m)
        id_copies.append(
            pltpu.make_async_remote_copy(
                src_ref=ids_ref.at[pl.ds(pl.multiple_of(dest * slot_cap, slot_cap), slot_cap), :],
                dst_ref=ids_out.at[pl.ds(pl.multiple_of(g * slot_cap, slot_cap), slot_cap), :],
                send_sem=id_s.at[m - 1],
                recv_sem=id_r.at[m - 1],
                device_id=(f, dest),
                device_id_type=MESH,
            )
        )
        id_copies[-1].start()
    own_ids = pl.ds(pl.multiple_of(g * slot_cap, slot_cap), slot_cap)
    ids_out[own_ids, :] = ids_ref[own_ids, :]

    step = 64

    def taps(first, pre_ref, dilation):
        for i in range(seq // step):
            rows = slice(i * step, (i + 1) * step)
            z = pre_ref[rows, :].astype(jnp.float32)
            s = jax.nn.sigmoid(z)
            grad_rows = first[rows, :].astype(jnp.float32)
            d = (grad_rows * s * (1.0 + z * (1.0 - s))).astype(jnp.bfloat16)
            dsh[1, rows, :] = d
            pad[PAD + i * step : PAD + (i + 1) * step, :] = d.astype(jnp.float32)
        for i in range(seq // step):
            rows = slice(i * step, (i + 1) * step)
            low = PAD + i * step
            dsh[0, rows, :] = pad[low + dilation : low + dilation + step, :].astype(jnp.bfloat16)
            dsh[2, rows, :] = pad[low - dilation : low - dilation + step, :].astype(jnp.bfloat16)

    def product(layer, rows, wrows):
        total = None
        for k in range(3):
            one = lax.dot_general(
                dsh[k, rows, :],
                wfull[layer, k, wrows, :],
                (((1,), (1,)), ((), ())),
                preferred_element_type=jnp.float32,
            )
            total = one if total is None else total + one
        return total

    mrows = seq // 2

    def live_of(i):
        spots = lax.broadcasted_iota(jnp.int32, (mrows, 1), 0) + i * mrows
        return (spots < len_ref[0]).astype(jnp.float32)

    taps(go_ref, p2_ref, 2)
    near(0, 0)
    near(0, 1)
    start_directs(1)
    far(0)
    for n, dest in enumerate((f, fx, fy, fd)):
        if n == 1:
            upper(0)
            near(1, 0)
        if n == 3:
            near(1, 1)
        if n > 0:
            shard_ready(0, n - 1)
        wrows = pl.ds(pl.multiple_of(dest * cols, cols), cols)
        for i in range(2):
            rows = slice(i * mrows, (i + 1) * mrows)
            grad[rows, wrows] = go_ref[rows, wrows].astype(jnp.float32) + live_of(i) * product(
                0, rows, wrows
            )
    far(1)
    taps(grad, p1_ref, 1)

    feat_copies = []
    for n, dest in enumerate((f, fx, fy, fd)):
        if n == 1:
            upper(1)
        if n > 0:
            shard_ready(1, n - 1)
        wrows = pl.ds(pl.multiple_of(dest * cols, cols), cols)
        for i in range(2):
            rows = slice(i * mrows, (i + 1) * mrows)
            live = live_of(i)
            full = grad[rows, wrows] + live * product(1, rows, wrows)
            full = (live * full).astype(jnp.bfloat16)
            full = full.reshape(mrows // BLK, BLK, cols)
            spots = pl.ds(i * (mrows // BLK), mrows // BLK)
            if n > 0:
                rg[n - 1, spots] = full
            else:
                gcols[pl.ds(f * (seq // BLK) + i * (mrows // BLK), mrows // BLK)] = full
        if n > 0:
            copy = pltpu.make_async_remote_copy(
                src_ref=rg.at[n - 1],
                dst_ref=gcols.at[pl.ds(f * (seq // BLK), seq // BLK)],
                send_sem=feat_s.at[n - 1],
                recv_sem=feat_r.at[n - 1],
                device_id=(dest, g),
                device_id_type=MESH,
            )
            copy.start()
            feat_copies.append(copy)
    src_copy.wait()
    for copy in feat_copies:
        copy.wait()

    order = [m for m in range(owner_count - 1, 0, -1)]
    order = sorted(order, key=lambda m: -(m // 2))
    row_copies = []
    for m in order:
        dest = flip(g, m)

        def pick(s, c, dest=dest, m=m):
            src = src_ref[dest * slot_cap + s, 0]
            send[m, s] = gcols[src]
            return c

        lax.fori_loop(0, slot_cap, pick, 0, unroll=True)
        copy = pltpu.make_async_remote_copy(
            src_ref=send.at[m],
            dst_ref=rows_out.at[g],
            send_sem=row_s.at[m - 1],
            recv_sem=row_r.at[m - 1],
            device_id=(f, dest),
            device_id_type=MESH,
        )
        copy.start()
        row_copies.append(copy)

    def pick_own(s, c):
        src = src_ref[g * slot_cap + s, 0]
        rows_out[g, s] = gcols[src]
        return c

    lax.fori_loop(0, slot_cap, pick_own, 0, unroll=True)
    for copy in id_copies + row_copies:
        copy.wait()
    for l in two:
        for t in two:
            for w in two:
                for s in two:
                    directs[l][t][w][s].wait_send()
            for s in two:
                relays[l][t][s].wait_send()
        for i in three:
            alongs[l][i].wait_send()
            for t in three:
                forwards[l][t][i].wait_send()


def table_kernel(ids_ref, rows_ref, out_ref, wide, *tables):
    slots = ids_ref.shape[0]
    chunk = out_ref.shape[1]

    @pl.when(pl.program_id(0) == 0)
    def _():
        def clear(i, c):
            spot = pl.ds(pl.multiple_of(i * 128, 128), 128)
            for table in tables:
                table[spot, :] = jnp.zeros((128, table.shape[1]), jnp.float32)
            return c

        lax.fori_loop(0, ROWS_OWN // 128, clear, 0)

        def add_slot(s, c):
            @pl.when(ids_ref[s, 0] >= 0)
            def _():
                base = pl.multiple_of(s * BLK, BLK)
                wide[...] = rows_ref[pl.ds(base, BLK), :].astype(jnp.float32)
                for r in range(0, BLK, TABLES):
                    spots = [pl.ds(ids_ref[s, r + q], 1) for q in range(TABLES)]
                    olds = [tables[q][spots[q], :] for q in range(TABLES)]
                    for q in range(TABLES):
                        tables[q][spots[q], :] = olds[q] + wide[r + q : r + q + 1, :]

            return c

        lax.fori_loop(0, slots, add_slot, 0)

    spot = pl.ds(pl.multiple_of(pl.program_id(0) * chunk, chunk), chunk)
    total = tables[0][spot, :]
    for table in tables[1:]:
        total = total + table[spot, :]
    out_ref[...] = total.T


def fused_body(grad_out, pre_first, pre_second, conv_first, conv_second, lengths, item_ids, owners):
    seq, width = grad_out.shape[1:]
    cols = conv_first.shape[1]
    owner_count = lax.axis_size("grp")
    blocks = owners.shape[0]
    slot_cap = max(2, 2 * blocks // owner_count)
    slots = owner_count * slot_cap
    smem = pl.BlockSpec(memory_space=pltpu.SMEM)
    vmem = pl.BlockSpec(memory_space=pltpu.VMEM)
    dma = pltpu.SemaphoreType.DMA
    bf16 = jnp.bfloat16
    rows, ids = pl.pallas_call(
        functools.partial(exchange_kernel, slot_cap, owner_count),
        out_shape=(
            jax.ShapeDtypeStruct((owner_count, slot_cap, BLK, cols), bf16),
            jax.ShapeDtypeStruct((slots, 4 * BLK), jnp.int32),
        ),
        in_specs=[smem] + [vmem] * 7,
        out_specs=(vmem, vmem),
        scratch_shapes=[
            pltpu.VMEM((2, 3, width, width), bf16),
            pltpu.VMEM((seq + 2 * PAD, width), jnp.float32),
            pltpu.VMEM((3, seq, width), bf16),
            pltpu.VMEM((seq, width), jnp.float32),
            pltpu.VMEM((3, seq // BLK, BLK, cols), bf16),
            pltpu.VMEM((4 * seq // BLK, BLK, cols), bf16),
            pltpu.VMEM((owner_count, slot_cap, BLK, cols), bf16),
            dma((2, 2, 2, 2)),
            dma((2, 2, 2, 2)),
            dma((2, 2, 2)),
            dma((2, 2, 2)),
            dma((2, 3)),
            dma((2, 3)),
            dma((2, 3, 3)),
            dma((2, 3, 3)),
            dma((3,)),
            dma((3,)),
            dma((owner_count - 1,)),
            dma((owner_count - 1,)),
            dma((owner_count - 1,)),
            dma((owner_count - 1,)),
            pltpu.VMEM((slots, 4 * BLK), jnp.int32),
            pltpu.VMEM((slots, 4 * BLK), jnp.int32),
            pltpu.SMEM((slots, 4 * BLK), jnp.int32),
            dma,
        ],
        compiler_params=pltpu.CompilerParams(collective_id=0, has_side_effects=True),
    )(
        lengths,
        owners.reshape(1, blocks),
        item_ids.reshape(blocks // 4, 4 * BLK),
        grad_out.reshape(seq, width),
        pre_first.reshape(seq, width),
        pre_second.reshape(seq, width),
        conv_first,
        conv_second,
    )
    chunk = 4096
    return pl.pallas_call(
        table_kernel,
        grid=(ROWS_OWN // chunk,),
        out_shape=jax.ShapeDtypeStruct((cols, ROWS_OWN), jnp.float32),
        in_specs=[smem, pl.BlockSpec((slots * BLK, cols), lambda i: (0, 0))],
        out_specs=pl.BlockSpec((cols, chunk), lambda i: (0, i)),
        scratch_shapes=[pltpu.VMEM((BLK, cols), jnp.float32)]
        + [pltpu.VMEM((ROWS_OWN, cols), jnp.float32)] * TABLES,
    )(ids, rows.reshape(slots * BLK, cols))


def layer_back(gradient, pre_acts, live_rows, dilation, product):
    seq_len = gradient.shape[0]
    pre_float = pre_acts.astype(jnp.float32)
    sig_val = jax.nn.sigmoid(pre_float)
    deltas = (gradient * sig_val * (1.0 + pre_float * (1.0 - sig_val))).astype(jnp.bfloat16)
    padded = jnp.pad(deltas, ((dilation, dilation), (0, 0)))
    tap_rows = jnp.stack(
        [
            padded[2 * dilation : 2 * dilation + seq_len],
            padded[dilation : dilation + seq_len],
            padded[0:seq_len],
        ]
    )
    return gradient + live_rows * product(tap_rows)


def gathered_product(weights):

    def apply_taps(tap_rows):
        return jnp.einsum(
            "ktd,kpd->tp",
            tap_rows,
            lax.all_gather(weights, "fsdp", axis=1, tiled=True),
            preferred_element_type=jnp.float32,
        )

    return apply_taps


def body(grad_out, pre_first, pre_second, conv_first, conv_second, lengths, item_ids, owners):
    seq_len = grad_out.shape[1]
    positions = jnp.arange(seq_len, dtype=jnp.int32)
    live_rows = (positions < lengths[0]).astype(jnp.float32)[:, None]
    gradient = grad_out[0].astype(jnp.float32)
    gradient = layer_back(gradient, pre_second[0], live_rows, 2, gathered_product(conv_second))
    gradient = layer_back(gradient, pre_first[0], live_rows, 1, gathered_product(conv_first))
    row_grad = (live_rows * gradient).astype(jnp.bfloat16)
    group_cols = lax.all_to_all(row_grad.T, "fsdp", split_axis=0, concat_axis=1, tiled=True)
    feat_cols = group_cols.shape[0]
    owner_count = lax.axis_size("grp")
    blocks = owners.shape[0]
    slot_cap = max(2, 2 * blocks // owner_count)
    block_dest = owners[:, 0]
    dest_hits = (block_dest[:, None] == jnp.arange(owner_count, dtype=jnp.int32)[None, :]).astype(
        jnp.int32
    )
    earlier = jnp.cumsum(dest_hits, axis=0) - dest_hits
    block_rank = jnp.sum(dest_hits * earlier, axis=1)
    slot_index = block_dest * slot_cap + block_rank
    select_int = (
        slot_index[:, None] == jnp.arange(owner_count * slot_cap, dtype=jnp.int32)[None, :]
    ).astype(jnp.int32)
    select_int = select_int.reshape(blocks, owner_count, slot_cap)
    select_map = select_int.astype(jnp.bfloat16)
    block_cols = group_cols.reshape(feat_cols, blocks, BLK)
    send_rows = jnp.einsum(
        "cbr,bos->ocsr", block_cols, select_map, preferred_element_type=jnp.float32
    )
    send_rows = send_rows.astype(jnp.bfloat16).reshape(owner_count, feat_cols, slot_cap * BLK)
    shifted_ids = item_ids.reshape(blocks, BLK) + 1
    send_ids = jnp.einsum("br,bos->osr", shifted_ids, select_int) - 1
    send_ids = send_ids.reshape(owner_count, slot_cap * BLK)
    recv_rows, recv_ids = (
        lax.all_to_all(send_rows, "grp", split_axis=0, concat_axis=0, tiled=True),
        lax.all_to_all(send_ids, "grp", split_axis=0, concat_axis=0, tiled=True),
    )
    flat_rows = jnp.transpose(recv_rows, (0, 2, 1)).reshape(-1, feat_cols).astype(jnp.float32)
    safe_ids = jnp.where(recv_ids < 0, ROWS_OWN, recv_ids).reshape(-1)
    summed = jax.ops.segment_sum(flat_rows, safe_ids, num_segments=ROWS_OWN + 1)
    return summed[:ROWS_OWN].T


def solution(mesh):
    fused = mesh.shape["fsdp"] == 4 and mesh.shape["grp"] == 8
    placed = (
        P(("fsdp", "grp"), None, None),
        P(("fsdp", "grp"), None, None),
        P(("fsdp", "grp"), None, None),
        P(None, "fsdp", None),
        P(None, "fsdp", None),
        P(("fsdp", "grp")),
        P("grp"),
        P("grp", None),
    )
    return jax.shard_map(
        fused_body if fused else body, mesh=mesh, in_specs=placed, out_specs=P("fsdp", "grp"), check_vma=False
    )
```

```python
import functools

import jax
import jax.numpy as jnp
from jax import lax
from jax.experimental import pallas as pl
from jax.experimental.pallas import tpu as pltpu
from jax.sharding import PartitionSpec as P

MESH = pl.DeviceIdType.MESH
BLK = 32
ROWS_OWN = 8192
PAD = 8
TABLES = 4


def flip(index, mask):
    out = 0
    for bit in range(6):
        have = (index // (1 << bit)) % 2
        out = out + ((1 - have) if (mask >> bit) & 1 else have) * (1 << bit)
    return out


def slot_plan(slot_cap, slots, own_row, ids_ref):
    blocks = own_row.shape[1]
    early = lax.broadcasted_iota(jnp.int32, (blocks, blocks), 0)
    late = lax.broadcasted_iota(jnp.int32, (blocks, blocks), 1)
    own_late = jnp.broadcast_to(own_row, (blocks, blocks))
    own_early = jnp.sum(jnp.where(early == late, own_late, 0), axis=1, keepdims=True)
    same = (own_early == own_late) & (early < late)
    rank = jnp.sum(jnp.where(same, 1, 0), axis=0, keepdims=True)
    slot = own_row * slot_cap + rank
    hit = slot == lax.broadcasted_iota(jnp.int32, (slots, blocks), 0)
    index = lax.broadcasted_iota(jnp.int32, (slots, blocks), 1)
    source = jnp.sum(jnp.where(hit, index, 0), axis=1, keepdims=True)
    used = jnp.sum(jnp.where(hit, 1, 0), axis=1, keepdims=True)
    lanes = ids_ref.shape[1]
    row_of = jnp.broadcast_to(source >> 2, (slots, lanes))
    lane_of = jnp.broadcast_to(source & 3, (slots, lanes))
    used = jnp.broadcast_to(used, (slots, lanes))
    ids = jnp.zeros((slots, lanes), jnp.int32)
    for r in range(ids_ref.shape[0]):
        ids = jnp.where(row_of == r, ids_ref[r : r + 1, :], ids)
    out = ids
    for q in range(1, 4):
        out = jnp.where(lane_of == q, pltpu.roll(ids, lanes - q * BLK, 1), out)
    return jnp.broadcast_to(source, (slots, lanes)), jnp.where(used > 0, out, -1)


def exchange_kernel(
    slot_cap,
    owner_count,
    len_ref,
    own_ref,
    item_ref,
    go_ref,
    p1_ref,
    p2_ref,
    w1_ref,
    w2_ref,
    rows_out,
    ids_out,
    wfull,
    pad,
    dsh,
    grad,
    rg,
    gcols,
    send,
    dir_s,
    dir_r,
    rel_s,
    rel_r,
    up_s,
    up_r,
    fw_s,
    fw_r,
    feat_s,
    feat_r,
    row_s,
    row_r,
    id_s,
    id_r,
    ids_ref,
    src_vmem,
    src_ref,
    src_sem,
):
    f = lax.axis_index("fsdp")
    g = lax.axis_index("grp")
    core = g % 2
    seq = grad.shape[0]
    width = grad.shape[1]
    cols = width // 4
    half = cols // 2
    quarter = cols // 4
    fx, fy, fd = flip(f, 1), flip(f, 2), flip(f, 3)
    mate = flip(g, 1)
    level = flip(g, 2)
    first_tap = 1 + (g // 2) % 2
    tap_of = (first_tap, 0, 3 - first_tap)

    barrier = pltpu.get_barrier_semaphore()
    for peer in (fx, fy, fd):
        pl.semaphore_signal(barrier, inc=1, device_id=(peer, g), device_id_type=MESH)
    for m in range(1, owner_count):
        pl.semaphore_signal(barrier, inc=1, device_id=(f, flip(g, m)), device_id_type=MESH)
    pad[0:PAD, :] = jnp.zeros((PAD, width), jnp.float32)
    pad[PAD + seq : 2 * PAD + seq, :] = jnp.zeros((PAD, width), jnp.float32)
    own_cols = pl.ds(pl.multiple_of(f * cols, cols), cols)
    wfull[0, :, own_cols, :] = w2_ref[...]
    wfull[1, :, own_cols, :] = w1_ref[...]
    pl.semaphore_wait(barrier, 3 + owner_count - 1)

    w_refs = (w2_ref, w1_ref)

    def part(layer, turn, owner, off, rows):
        spot = pl.ds(pl.multiple_of(owner * cols + off, quarter), rows)
        return wfull.at[layer, tap_of[turn], spot, :]

    def move(src, dst, send_sem, recv_sem, peer):
        return pltpu.make_async_remote_copy(
            src_ref=src,
            dst_ref=dst,
            send_sem=send_sem,
            recv_sem=recv_sem,
            device_id=peer,
            device_id_type=MESH,
        )

    def direct(layer, turn, way, sub):
        off = core * half + sub * quarter
        spot = pl.ds(pl.multiple_of(off, quarter), quarter)
        at = (layer, turn, way, sub)
        return move(
            w_refs[layer].at[tap_of[turn], spot, :],
            part(layer, turn, f, off, quarter),
            dir_s.at[at],
            dir_r.at[at],
            ((fx, fy)[way], g),
        )

    def relay(layer, turn, sub):
        holder, peer = ((fx, fy), (fy, fx))[sub]
        place = part(layer, turn, holder, core * half + sub * quarter, quarter)
        at = (layer, turn, sub)
        return move(place, place, rel_s.at[at], rel_r.at[at], (peer, g))

    def along(layer, which):
        place = part(layer, 0, (fx, fy, fd)[which], core * half, half)
        at = (layer, which)
        return move(place, place, up_s.at[at], up_r.at[at], (f, level))

    def forward(layer, turn, which):
        place = part(layer, turn, (fx, fy, fd)[which], core * half, half)
        at = (layer, turn, which)
        return move(place, place, fw_s.at[at], fw_r.at[at], (f, mate))

    two, three = range(2), range(3)
    directs = [[[[direct(l, t, w, s) for s in two] for w in two] for t in two] for l in two]
    relays = [[[relay(l, t, s) for s in two] for t in two] for l in two]
    alongs = [[along(l, i) for i in three] for l in two]
    forwards = [[[forward(l, t, i) for i in three] for t in three] for l in two]

    def start_directs(layer):
        for turn in two:
            directs[layer][turn][0][0].start()
            directs[layer][turn][1][1].start()
            directs[layer][turn][0][1].start()
            directs[layer][turn][1][0].start()

    def near(layer, turn):
        directs[layer][turn][0][0].wait_recv()
        relays[layer][turn][0].start()
        directs[layer][turn][1][1].wait_recv()
        relays[layer][turn][1].start()
        for way in two:
            directs[layer][turn][way][1 - way].wait_recv()
            if turn == 0:
                alongs[layer][way].start()
            forwards[layer][turn][way].start()

    def far(layer):
        for turn in two:
            relays[layer][turn][0].wait_recv()
            relays[layer][turn][1].wait_recv()
            if turn == 0:
                alongs[layer][2].start()
            forwards[layer][turn][2].start()

    def upper(layer, which_ones):
        for which in which_ones:
            alongs[layer][which].wait_recv()
            forwards[layer][2][which].start()

    def shard_ready(layer, which):
        for turn in three:
            forwards[layer][turn][which].wait_recv()

    start_directs(0)
    source, send_ids = slot_plan(slot_cap, owner_count * slot_cap, own_ref[...], item_ref)
    ids_ref[...] = send_ids
    src_vmem[...] = source
    src_copy = pltpu.make_async_copy(src_vmem, src_ref, src_sem)
    src_copy.start()

    id_copies = []
    for m in range(1, owner_count):
        dest = flip(g, m)
        id_copies.append(
            pltpu.make_async_remote_copy(
                src_ref=ids_ref.at[pl.ds(pl.multiple_of(dest * slot_cap, slot_cap), slot_cap), :],
                dst_ref=ids_out.at[pl.ds(pl.multiple_of(g * slot_cap, slot_cap), slot_cap), :],
                send_sem=id_s.at[m - 1],
                recv_sem=id_r.at[m - 1],
                device_id=(f, dest),
                device_id_type=MESH,
            )
        )
        id_copies[-1].start()
    own_ids = pl.ds(pl.multiple_of(g * slot_cap, slot_cap), slot_cap)
    ids_out[own_ids, :] = ids_ref[own_ids, :]

    step = 64

    def taps(first, pre_ref, dilation):
        for i in range(seq // step):
            rows = slice(i * step, (i + 1) * step)
            z = pre_ref[rows, :].astype(jnp.float32)
            s = jax.nn.sigmoid(z)
            grad_rows = first[rows, :].astype(jnp.float32)
            d = (grad_rows * s * (1.0 + z * (1.0 - s))).astype(jnp.bfloat16)
            dsh[1, rows, :] = d
            pad[PAD + i * step : PAD + (i + 1) * step, :] = d.astype(jnp.float32)
        for i in range(seq // step):
            rows = slice(i * step, (i + 1) * step)
            low = PAD + i * step
            dsh[0, rows, :] = pad[low + dilation : low + dilation + step, :].astype(jnp.bfloat16)
            dsh[2, rows, :] = pad[low - dilation : low - dilation + step, :].astype(jnp.bfloat16)

    def product(layer, rows, wrows):
        total = None
        for k in range(3):
            one = lax.dot_general(
                dsh[k, rows, :],
                wfull[layer, k, wrows, :],
                (((1,), (1,)), ((), ())),
                preferred_element_type=jnp.float32,
            )
            total = one if total is None else total + one
        return total

    mrows = seq // 2

    def live_of(i):
        spots = lax.broadcasted_iota(jnp.int32, (mrows, 1), 0) + i * mrows
        return (spots < len_ref[0]).astype(jnp.float32)

    taps(go_ref, p2_ref, 2)
    near(0, 0)
    near(0, 1)
    start_directs(1)
    far(0)
    for n, dest in enumerate((f, fx, fy, fd)):
        if n == 1:
            upper(0, (0, 1))
            near(1, 0)
        if n == 2:
            upper(0, (2,))
        if n == 3:
            near(1, 1)
        if n > 0:
            shard_ready(0, n - 1)
        wrows = pl.ds(pl.multiple_of(dest * cols, cols), cols)
        for i in range(2):
            rows = slice(i * mrows, (i + 1) * mrows)
            grad[rows, wrows] = go_ref[rows, wrows].astype(jnp.float32) + live_of(i) * product(
                0, rows, wrows
            )
    far(1)
    taps(grad, p1_ref, 1)

    feat_copies = []
    for n, dest in enumerate((f, fx, fy, fd)):
        if n == 1:
            upper(1, (0, 1))
        if n == 2:
            upper(1, (2,))
        if n > 0:
            shard_ready(1, n - 1)
        wrows = pl.ds(pl.multiple_of(dest * cols, cols), cols)
        for i in range(2):
            rows = slice(i * mrows, (i + 1) * mrows)
            live = live_of(i)
            full = grad[rows, wrows] + live * product(1, rows, wrows)
            full = (live * full).astype(jnp.bfloat16)
            full = full.reshape(mrows // BLK, BLK, cols)
            spots = pl.ds(i * (mrows // BLK), mrows // BLK)
            if n > 0:
                rg[n - 1, spots] = full
            else:
                gcols[pl.ds(f * (seq // BLK) + i * (mrows // BLK), mrows // BLK)] = full
        if n > 0:
            copy = pltpu.make_async_remote_copy(
                src_ref=rg.at[n - 1],
                dst_ref=gcols.at[pl.ds(f * (seq // BLK), seq // BLK)],
                send_sem=feat_s.at[n - 1],
                recv_sem=feat_r.at[n - 1],
                device_id=(dest, g),
                device_id_type=MESH,
            )
            copy.start()
            feat_copies.append(copy)
    src_copy.wait()
    for copy in feat_copies:
        copy.wait()

    order = [m for m in range(owner_count - 1, 0, -1)]
    order = sorted(order, key=lambda m: -(m // 2))
    row_copies = []
    for m in order:
        dest = flip(g, m)

        def pick(s, c, dest=dest, m=m):
            src = src_ref[dest * slot_cap + s, 0]
            send[m, s] = gcols[src]
            return c

        lax.fori_loop(0, slot_cap, pick, 0, unroll=True)
        copy = pltpu.make_async_remote_copy(
            src_ref=send.at[m],
            dst_ref=rows_out.at[g],
            send_sem=row_s.at[m - 1],
            recv_sem=row_r.at[m - 1],
            device_id=(f, dest),
            device_id_type=MESH,
        )
        copy.start()
        row_copies.append(copy)

    def pick_own(s, c):
        src = src_ref[g * slot_cap + s, 0]
        rows_out[g, s] = gcols[src]
        return c

    lax.fori_loop(0, slot_cap, pick_own, 0, unroll=True)
    for copy in id_copies + row_copies:
        copy.wait()
    for l in two:
        for t in two:
            for w in two:
                for s in two:
                    directs[l][t][w][s].wait_send()
            for s in two:
                relays[l][t][s].wait_send()
        for i in three:
            alongs[l][i].wait_send()
            for t in three:
                forwards[l][t][i].wait_send()


def table_kernel(ids_ref, rows_ref, out_ref, wide, *tables):
    slots = ids_ref.shape[0]
    chunk = out_ref.shape[1]

    @pl.when(pl.program_id(0) == 0)
    def _():
        def clear(i, c):
            spot = pl.ds(pl.multiple_of(i * 128, 128), 128)
            for table in tables:
                table[spot, :] = jnp.zeros((128, table.shape[1]), jnp.float32)
            return c

        lax.fori_loop(0, ROWS_OWN // 128, clear, 0)

        def add_slot(s, c):
            @pl.when(ids_ref[s, 0] >= 0)
            def _():
                base = pl.multiple_of(s * BLK, BLK)
                wide[...] = rows_ref[pl.ds(base, BLK), :].astype(jnp.float32)
                for r in range(0, BLK, TABLES):
                    spots = [pl.ds(ids_ref[s, r + q], 1) for q in range(TABLES)]
                    olds = [tables[q][spots[q], :] for q in range(TABLES)]
                    for q in range(TABLES):
                        tables[q][spots[q], :] = olds[q] + wide[r + q : r + q + 1, :]

            return c

        lax.fori_loop(0, slots, add_slot, 0)

    spot = pl.ds(pl.multiple_of(pl.program_id(0) * chunk, chunk), chunk)
    total = tables[0][spot, :]
    for table in tables[1:]:
        total = total + table[spot, :]
    out_ref[...] = total.T


def fused_body(grad_out, pre_first, pre_second, conv_first, conv_second, lengths, item_ids, owners):
    seq, width = grad_out.shape[1:]
    cols = conv_first.shape[1]
    owner_count = lax.axis_size("grp")
    blocks = owners.shape[0]
    slot_cap = max(2, 2 * blocks // owner_count)
    slots = owner_count * slot_cap
    smem = pl.BlockSpec(memory_space=pltpu.SMEM)
    vmem = pl.BlockSpec(memory_space=pltpu.VMEM)
    dma = pltpu.SemaphoreType.DMA
    bf16 = jnp.bfloat16
    rows, ids = pl.pallas_call(
        functools.partial(exchange_kernel, slot_cap, owner_count),
        out_shape=(
            jax.ShapeDtypeStruct((owner_count, slot_cap, BLK, cols), bf16),
            jax.ShapeDtypeStruct((slots, 4 * BLK), jnp.int32),
        ),
        in_specs=[smem] + [vmem] * 7,
        out_specs=(vmem, vmem),
        scratch_shapes=[
            pltpu.VMEM((2, 3, width, width), bf16),
            pltpu.VMEM((seq + 2 * PAD, width), jnp.float32),
            pltpu.VMEM((3, seq, width), bf16),
            pltpu.VMEM((seq, width), jnp.float32),
            pltpu.VMEM((3, seq // BLK, BLK, cols), bf16),
            pltpu.VMEM((4 * seq // BLK, BLK, cols), bf16),
            pltpu.VMEM((owner_count, slot_cap, BLK, cols), bf16),
            dma((2, 2, 2, 2)),
            dma((2, 2, 2, 2)),
            dma((2, 2, 2)),
            dma((2, 2, 2)),
            dma((2, 3)),
            dma((2, 3)),
            dma((2, 3, 3)),
            dma((2, 3, 3)),
            dma((3,)),
            dma((3,)),
            dma((owner_count - 1,)),
            dma((owner_count - 1,)),
            dma((owner_count - 1,)),
            dma((owner_count - 1,)),
            pltpu.VMEM((slots, 4 * BLK), jnp.int32),
            pltpu.VMEM((slots, 4 * BLK), jnp.int32),
            pltpu.SMEM((slots, 4 * BLK), jnp.int32),
            dma,
        ],
        compiler_params=pltpu.CompilerParams(collective_id=0, has_side_effects=True),
    )(
        lengths,
        owners.reshape(1, blocks),
        item_ids.reshape(blocks // 4, 4 * BLK),
        grad_out.reshape(seq, width),
        pre_first.reshape(seq, width),
        pre_second.reshape(seq, width),
        conv_first,
        conv_second,
    )
    chunk = 4096
    return pl.pallas_call(
        table_kernel,
        grid=(ROWS_OWN // chunk,),
        out_shape=jax.ShapeDtypeStruct((cols, ROWS_OWN), jnp.float32),
        in_specs=[smem, pl.BlockSpec((slots * BLK, cols), lambda i: (0, 0))],
        out_specs=pl.BlockSpec((cols, chunk), lambda i: (0, i)),
        scratch_shapes=[pltpu.VMEM((BLK, cols), jnp.float32)]
        + [pltpu.VMEM((ROWS_OWN, cols), jnp.float32)] * TABLES,
    )(ids, rows.reshape(slots * BLK, cols))


def layer_back(gradient, pre_acts, live_rows, dilation, product):
    seq_len = gradient.shape[0]
    pre_float = pre_acts.astype(jnp.float32)
    sig_val = jax.nn.sigmoid(pre_float)
    deltas = (gradient * sig_val * (1.0 + pre_float * (1.0 - sig_val))).astype(jnp.bfloat16)
    padded = jnp.pad(deltas, ((dilation, dilation), (0, 0)))
    tap_rows = jnp.stack(
        [
            padded[2 * dilation : 2 * dilation + seq_len],
            padded[dilation : dilation + seq_len],
            padded[0:seq_len],
        ]
    )
    return gradient + live_rows * product(tap_rows)


def gathered_product(weights):

    def apply_taps(tap_rows):
        return jnp.einsum(
            "ktd,kpd->tp",
            tap_rows,
            lax.all_gather(weights, "fsdp", axis=1, tiled=True),
            preferred_element_type=jnp.float32,
        )

    return apply_taps


def body(grad_out, pre_first, pre_second, conv_first, conv_second, lengths, item_ids, owners):
    seq_len = grad_out.shape[1]
    positions = jnp.arange(seq_len, dtype=jnp.int32)
    live_rows = (positions < lengths[0]).astype(jnp.float32)[:, None]
    gradient = grad_out[0].astype(jnp.float32)
    gradient = layer_back(gradient, pre_second[0], live_rows, 2, gathered_product(conv_second))
    gradient = layer_back(gradient, pre_first[0], live_rows, 1, gathered_product(conv_first))
    row_grad = (live_rows * gradient).astype(jnp.bfloat16)
    group_cols = lax.all_to_all(row_grad.T, "fsdp", split_axis=0, concat_axis=1, tiled=True)
    feat_cols = group_cols.shape[0]
    owner_count = lax.axis_size("grp")
    blocks = owners.shape[0]
    slot_cap = max(2, 2 * blocks // owner_count)
    block_dest = owners[:, 0]
    dest_hits = (block_dest[:, None] == jnp.arange(owner_count, dtype=jnp.int32)[None, :]).astype(
        jnp.int32
    )
    earlier = jnp.cumsum(dest_hits, axis=0) - dest_hits
    block_rank = jnp.sum(dest_hits * earlier, axis=1)
    slot_index = block_dest * slot_cap + block_rank
    select_int = (
        slot_index[:, None] == jnp.arange(owner_count * slot_cap, dtype=jnp.int32)[None, :]
    ).astype(jnp.int32)
    select_int = select_int.reshape(blocks, owner_count, slot_cap)
    select_map = select_int.astype(jnp.bfloat16)
    block_cols = group_cols.reshape(feat_cols, blocks, BLK)
    send_rows = jnp.einsum(
        "cbr,bos->ocsr", block_cols, select_map, preferred_element_type=jnp.float32
    )
    send_rows = send_rows.astype(jnp.bfloat16).reshape(owner_count, feat_cols, slot_cap * BLK)
    shifted_ids = item_ids.reshape(blocks, BLK) + 1
    send_ids = jnp.einsum("br,bos->osr", shifted_ids, select_int) - 1
    send_ids = send_ids.reshape(owner_count, slot_cap * BLK)
    recv_rows, recv_ids = (
        lax.all_to_all(send_rows, "grp", split_axis=0, concat_axis=0, tiled=True),
        lax.all_to_all(send_ids, "grp", split_axis=0, concat_axis=0, tiled=True),
    )
    flat_rows = jnp.transpose(recv_rows, (0, 2, 1)).reshape(-1, feat_cols).astype(jnp.float32)
    safe_ids = jnp.where(recv_ids < 0, ROWS_OWN, recv_ids).reshape(-1)
    summed = jax.ops.segment_sum(flat_rows, safe_ids, num_segments=ROWS_OWN + 1)
    return summed[:ROWS_OWN].T


def solution(mesh):
    fused = mesh.shape["fsdp"] == 4 and mesh.shape["grp"] == 8
    placed = (
        P(("fsdp", "grp"), None, None),
        P(("fsdp", "grp"), None, None),
        P(("fsdp", "grp"), None, None),
        P(None, "fsdp", None),
        P(None, "fsdp", None),
        P(("fsdp", "grp")),
        P("grp"),
        P("grp", None),
    )
    return jax.shard_map(
        fused_body if fused else body, mesh=mesh, in_specs=placed, out_specs=P("fsdp", "grp"), check_vma=False
    )
```
